32 devices in a mesh: seq: 8 (over y, x, core), head: 4 (over z).
Axes of the slice: x: 2, y: 2, z: 4, core: 2. Of those that a mesh axis runs over, the one named last changes fastest.
Arguments:
- query_rows: bfloat16 [12288, 4096], P('seq', 'head'), may hold values from -8 to 8
- key_rows: bfloat16 [12288, 4096], P('seq', 'head'), may hold values from -8 to 8
- value_rows: bfloat16 [12288, 4096], P('seq', 'head'), may hold values from -6 to 6
- frame_lengths: int32 [8], P('seq'), may hold values from 512 to 1536, as said below
- step_rates: float32 [8, 8192], P('head', 'seq'), may hold values from 0.1 to 1
- fast_gate: float32 [8, 512, 512], P('head'), may hold values from -0.25 to 0.25
- fast_up: float32 [8, 512, 512], P('head'), may hold values from -0.25 to 0.25
- fast_down: float32 [8, 512, 512], P('head'), may hold values from -0.25 to 0.25
- output_weight: bfloat16 [4096, 4096], P('head'), may hold values from -0.09375 to 0.09375
Outputs:
- layer_output: bfloat16 [8192, 4096], P(('seq', 'head'))
The draws below stay inside these ranges and needn't reach their ends.
Inputs may be any that keep to these rules, and one draw needn't show every extreme that they name: `frame_lengths`: the lengths sum to 8192. For every shard s, offset[s] lies between s * 1024 and s * 1024 + 1024 // 2; in every draw some shard holds 1536 tokens and some offset reaches s * 1024 + 1024 // 2.
All inputs are finite; a program needn't handle non-finite values.
Results may differ from the reference program's by a relative error of at most 0.025.
Values may be sent and summed in bfloat16 or wider, within the bound.
A program may use at most 128 MiB of HBM per device.

```python
import math
import jax
import jax.numpy as jnp
from jax import lax

HEADS = 8
HD = 512
FH = 512
WINDOW = 512
ITERS = 2
TOK_DEV = 1024
D = 4096
TOKENS = 8192
CAP = 1536
FRAME_ROWS = 12288
N_SEQ = 8
N_HEAD = 4


def paired_rows(key):
    row_count = N_SEQ * CAP
    base_query = jax.random.normal(jax.random.fold_in(key, 11), (row_count, D), jnp.float32)
    base_key = jax.random.normal(jax.random.fold_in(key, 12), (row_count, D), jnp.float32)
    return (jnp.clip(base_query, -8.0, 8.0), jnp.clip(base_key, -8.0, 8.0))


def draw_query_rows(key, part):
    return paired_rows(key)[0].astype(jnp.bfloat16)


def draw_key_rows(key, part):
    return paired_rows(key)[1].astype(jnp.bfloat16)


def draw_frame_lengths(key, part):
    slack_rows = TOK_DEV // 2
    excess = jax.random.randint(jax.random.fold_in(key, 21), (N_SEQ,), 0, slack_rows + 1)
    chosen = jax.random.randint(jax.random.fold_in(key, 22), (), 1, N_SEQ - 1)
    excess = excess.at[chosen].set(slack_rows)
    excess = excess.at[chosen - 1].set(0)
    excess = excess.at[N_SEQ - 1].set(0)
    before = jnp.concatenate([jnp.zeros((1,), jnp.int32), excess[:-1].astype(jnp.int32)])
    return (TOK_DEV + excess.astype(jnp.int32) - before).astype(jnp.int32)


def block_scale(rng, extent, split, least, top_value):
    def one(axis_at, blocks):
        draws = jax.random.uniform(jax.random.fold_in(jax.random.fold_in(rng, 6), axis_at), (blocks,), jnp.float32, least / len(split), top_value / len(split))
        return jnp.repeat(jnp.exp(draws), extent[axis_at] // blocks).reshape((-1,) + (1,) * (len(extent) - axis_at - 1))

    gain = one(*split[0])
    for cut in split[1:]:
        gain = gain * one(*cut)
    return gain


def noise(own_key, shape, scale, bound, split=(), kind=jnp.bfloat16):
    loudness = block_scale(own_key, shape, split, -0.22, 0.18) if split else 1.0
    result = jax.random.normal(own_key, shape, jnp.float32) * scale * loudness
    return jnp.minimum(jnp.maximum(result, -bound), bound).astype(kind)


def setup_inputs(seed: int = 0) -> dict:
    splits = jax.random.split(jax.random.key(seed), 10)
    return {
        "query_rows": draw_query_rows(jax.random.fold_in(splits[9], 71), 0),
        "key_rows": draw_key_rows(jax.random.fold_in(splits[9], 71), 0),
        "value_rows": noise(splits[2], (FRAME_ROWS, D), 1.0, 6.0, ((0, 8), (1, 4))),
        "frame_lengths": draw_frame_lengths(jax.random.fold_in(splits[9], 71), 0),
        "step_rates": jnp.clip(jnp.exp(math.log(1.0) - 2.3025851 * jax.random.uniform(splits[4], (HEADS, TOKENS), jnp.float32) ** block_scale(splits[4], (HEADS, TOKENS), ((0, 4), (1, 8)), -0.2, 0.2)), 0.1, 1.0),
        "fast_gate": noise(splits[5], (HEADS, HD, FH), HD ** -0.5, 0.25, ((0, 4),), jnp.float32),
        "fast_up": noise(splits[6], (HEADS, HD, FH), HD ** -0.5, 0.25, ((0, 4),), jnp.float32),
        "fast_down": noise(splits[7], (HEADS, FH, HD), FH ** -0.5, 0.25, ((0, 4),), jnp.float32),
        "output_weight": noise(splits[8], (D, D), D ** -0.5, 0.09375, ((0, 4),)),
    }


poly_first = 3.4445
poly_second = -4.775
poly_third = 2.0315
epsilon = 1e-07
masked_score = -1e+30

def rounded(value):
    return lax.optimization_barrier(value.astype(jnp.bfloat16)).astype(jnp.float32)

def swish_slope(before_act):
    sigma = jax.nn.sigmoid(before_act)
    return sigma * (1.0 + before_act * (1.0 - sigma))

def orthogonal(gradient):
    norm_value = jnp.sqrt(lax.optimization_barrier(jnp.sum(gradient * gradient, axis=(1, 2), keepdims=True)))
    current = gradient / (norm_value + epsilon)
    for repeat in range(ITERS):
        gram_matrix = jnp.einsum('hrc,hsc->hrs', current, current, precision=lax.Precision.HIGHEST)
        polynomial = poly_second * gram_matrix + poly_third * jnp.einsum('hrs,hst->hrt', gram_matrix, gram_matrix, precision=lax.Precision.HIGHEST)
        current = poly_first * current + jnp.einsum('hrs,hsc->hrc', polynomial, current, precision=lax.Precision.HIGHEST)
    return current

def reference(query_rows, key_rows, value_rows, frame_lengths, step_rates, fast_gate, fast_up, fast_down, output_weight):
    lengths_int = frame_lengths.astype(jnp.int32)
    offsets = (jnp.cumsum(lengths_int) - lengths_int).astype(jnp.int32)
    row_index = jnp.arange(N_SEQ * CAP, dtype=jnp.int32)
    shard_index = row_index // CAP
    inside = row_index % CAP
    target_row = jnp.where(inside < lengths_int[shard_index], offsets[shard_index] + inside, TOKENS).astype(jnp.int32)

    def arrange(frame_rows):
        empty_rows = jnp.zeros((TOKENS, D), frame_rows.dtype)
        return empty_rows.at[target_row].set(frame_rows, mode='drop').reshape(TOKENS, HEADS, HD)
    queries = arrange(query_rows)
    keys_seq = arrange(key_rows)
    values_seq = arrange(value_rows)
    block_rows = TOK_DEV // 2
    key_pad = jnp.concatenate([jnp.zeros((WINDOW, HEADS, HD), keys_seq.dtype), keys_seq], axis=0)
    value_pad = jnp.concatenate([jnp.zeros((WINDOW, HEADS, HD), values_seq.dtype), values_seq], axis=0)
    scale_factor = 1.0 / math.sqrt(HD)

    def attend_block(block_id):
        first_row = block_id * block_rows
        query_block = lax.dynamic_slice_in_dim(queries, first_row, block_rows, 0).astype(jnp.float32)
        key_block = lax.dynamic_slice_in_dim(key_pad, first_row, block_rows + WINDOW, 0).astype(jnp.float32)
        value_block = lax.dynamic_slice_in_dim(value_pad, first_row, block_rows + WINDOW, 0).astype(jnp.float32)
        scores = jnp.einsum('qhd,khd->hqk', query_block, key_block) * scale_factor
        query_pos = first_row + jnp.arange(block_rows, dtype=jnp.int32)[:, None]
        key_pos = first_row - WINDOW + jnp.arange(block_rows + WINDOW, dtype=jnp.int32)[None, :]
        allowed = (key_pos <= query_pos) & (key_pos > query_pos - WINDOW) & (key_pos >= 0)
        scores = jnp.where(allowed[None], scores, masked_score)
        row_peak = lax.optimization_barrier(jnp.max(scores, axis=2, keepdims=True))
        weights = jnp.exp(scores - row_peak)
        totals = lax.optimization_barrier(jnp.sum(weights, axis=2))
        summed = jnp.einsum('hqk,khd->qhd', rounded(weights), value_block)
        return (summed / jnp.transpose(totals)[:, :, None]).astype(jnp.bfloat16)
    attention = lax.map(attend_block, jnp.arange(TOKENS // block_rows, dtype=jnp.int32)).reshape(TOKENS, HEADS, HD)
    gate_low = rounded(fast_gate)
    up_low = rounded(fast_up)
    down_low = rounded(fast_down)
    keys_wide = keys_seq.astype(jnp.float32)
    pre_gate = jnp.einsum('nhd,hdf->nhf', keys_wide, gate_low)
    pre_up = jnp.einsum('nhd,hdf->nhf', keys_wide, up_low)
    activated = jax.nn.silu(pre_gate)
    inner = rounded(activated * pre_up)
    target = rounded(-jnp.transpose(step_rates)[:, :, None] * values_seq.astype(jnp.float32))
    grad_down = jnp.einsum('nhf,nhd->hfd', inner, target)
    back = jnp.einsum('nhd,hfd->nhf', target, down_low)
    back_up = rounded(back * activated)
    back_gate = rounded(back * pre_up * swish_slope(pre_gate))
    grad_gate = jnp.einsum('nhd,nhf->hdf', keys_wide, back_gate)
    grad_up = jnp.einsum('nhd,nhf->hdf', keys_wide, back_up)
    new_gate = rounded(fast_gate - orthogonal(grad_gate))
    new_up = rounded(fast_up - orthogonal(grad_up))
    new_down = rounded(fast_down - orthogonal(grad_down))
    queries_wide = queries.astype(jnp.float32)
    apply_gate = jnp.einsum('nhd,hdf->nhf', queries_wide, new_gate)
    apply_up = jnp.einsum('nhd,hdf->nhf', queries_wide, new_up)
    middle = rounded(jax.nn.silu(apply_gate) * apply_up)
    fast_out = jnp.einsum('nhf,hfd->nhd', middle, new_down)
    combined = (attention.astype(jnp.float32) + fast_out).astype(jnp.bfloat16).reshape(TOKENS, D)
    group_cols = D // N_HEAD
    summed_out = jnp.zeros((TOKENS, D), jnp.float32)
    for member in range(N_HEAD):
        partial_value = jnp.dot(combined[:, member * group_cols:(member + 1) * group_cols], output_weight[member * group_cols:(member + 1) * group_cols], preferred_element_type=jnp.float32)
        summed_out = summed_out + rounded(partial_value)
    return summed_out.astype(jnp.bfloat16)
```

```python
import math

import jax
import jax.numpy as jnp
from jax import lax
from jax.sharding import PartitionSpec as P

HD = 512
WINDOW = 512
ITERS = 2

poly_first = 3.4445
poly_second = -4.775
poly_third = 2.0315
epsilon = 1e-07
masked_score = -1e30
bf16 = jnp.bfloat16
f32 = jnp.float32


def mm(a, b, dims=((1,), (0,))):
    return lax.dot_general(a, b, (dims, ((), ())), preferred_element_type=f32)


def swap(value, axis, mask):
    count = lax.axis_size(axis)
    return lax.ppermute(value, axis, [(i, i ^ mask) for i in range(count)])


def shifted(value, axis, steps):
    count = lax.axis_size(axis)
    first, last = (max(0, -steps), min(count, count - steps))
    return lax.ppermute(value, axis, [(i, i + steps) for i in range(first, last)])


def bit_of(axis, mask):
    return (lax.axis_index(axis) & mask) != 0


def halves(value, dim, high):
    half = value.shape[dim] // 2
    low_part = lax.slice_in_dim(value, 0, half, axis=dim)
    high_part = lax.slice_in_dim(value, half, 2 * half, axis=dim)
    return jnp.where(high, high_part, low_part), jnp.where(high, low_part, high_part)


def joined(mine, other, dim, high):
    return jnp.concatenate(
        [jnp.where(high, other, mine), jnp.where(high, mine, other)], axis=dim
    )


def reduce_over(value, masks, dim):
    for mask in masks:
        keep, give = halves(value, dim, bit_of("seq", mask))
        value = keep.astype(f32) + swap(give.astype(bf16), "seq", mask).astype(f32)
    return value.astype(bf16)


def gather_over(value, masks, dim):
    for mask in masks:
        value = joined(value, swap(value, "seq", mask), dim, bit_of("seq", mask))
    return value


def seq_sum(value, masks):
    half = value.shape[2] // 2
    parts = []
    for part, order in ((value[:, :, :half], masks), (value[:, :, half:], masks[::-1])):
        part = reduce_over(part, order, 1)
        parts.append(gather_over(part, order[::-1], 1))
    return jnp.concatenate(parts, axis=2).astype(f32)


def orthogonal(gradient):
    norm_value = jnp.sqrt(jnp.sum(gradient * gradient, axis=(1, 2), keepdims=True))
    current = gradient / (norm_value + epsilon)
    for repeat in range(ITERS):
        low = current.astype(bf16)
        gram = jnp.einsum("hrc,hsc->hrs", low, low, preferred_element_type=f32)
        gram_low = gram.astype(bf16)
        poly = poly_second * gram + poly_third * jnp.einsum(
            "hrs,hst->hrt", gram_low, gram_low, preferred_element_type=f32
        )
        current = poly_first * current + jnp.einsum(
            "hrs,hsc->hrc", poly.astype(bf16), low, preferred_element_type=f32
        )
    return current


def head_grads(key, value, rate, gate, up, down):
    pre_gate = mm(key, gate)
    pre_up = mm(key, up)
    sigma = jax.nn.sigmoid(pre_gate)
    activated = pre_gate * sigma
    inner = (activated * pre_up).astype(bf16)
    target = (rate * value.astype(f32)).astype(bf16)
    grad_down = mm(inner, target, ((0,), (0,)))
    back = mm(target, down, ((1,), (1,)))
    back_up = (back * activated).astype(bf16)
    back_gate = (back * pre_up * (sigma * (1.0 + pre_gate * (1.0 - sigma)))).astype(bf16)
    return [mm(key, back_gate, ((0,), (0,))), mm(key, back_up, ((0,), (0,))), grad_down]


def attend(query, key_ext, value_ext, halo_live, block_rows):
    scale_factor = 1.0 / math.sqrt(HD)
    pieces = []
    for first in range(0, query.shape[0], block_rows):
        span = block_rows + WINDOW
        scores = (
            mm(query[first : first + block_rows], key_ext[first : first + span], ((1,), (1,)))
            * scale_factor
        )
        query_pos = first + lax.broadcasted_iota(jnp.int32, (block_rows, 1), 0)
        key_pos = first - WINDOW + lax.broadcasted_iota(jnp.int32, (1, span), 1)
        allowed = (
            (key_pos <= query_pos) & (key_pos > query_pos - WINDOW) & ((key_pos >= 0) | halo_live)
        )
        scores = jnp.where(allowed, scores, masked_score)
        weights = jnp.exp(scores - jnp.max(scores, axis=1, keepdims=True))
        totals = jnp.sum(weights, axis=1, keepdims=True)
        summed = mm(weights.astype(bf16), value_ext[first : first + span])
        pieces.append((summed / totals).astype(bf16))
    return jnp.concatenate(pieces, axis=0)


def seq_gather(piece, masks):
    half = piece.shape[1] // 2
    parts = []
    for part, order in ((piece[:, :half], masks), (piece[:, half:], masks[::-1])):
        slot = part[None]
        for mask in order:
            slot = jnp.concatenate([slot, swap(slot, "seq", mask)], axis=0)
        parts.append(slot)
    return parts


def per_device(
    query_rows,
    key_rows,
    value_rows,
    frame_lengths,
    step_rates,
    fast_gate,
    fast_up,
    fast_down,
    output_weight,
):
    local_heads = query_rows.shape[1] // HD
    cap = query_rows.shape[0]
    tok = step_rates.shape[1]
    slack = cap - tok
    n_seq, n_head = lax.axis_size("seq"), lax.axis_size("head")
    seq_index = lax.axis_index("seq")
    head_index = lax.axis_index("head")
    masks = [1 << b for b in range(1, n_seq.bit_length() - 1)]

    lengths = lax.all_gather(frame_lengths, "seq", tiled=True)
    before = lax.broadcasted_iota(jnp.int32, (n_seq,), 0) < seq_index
    drift = jnp.sum(jnp.where(before, lengths, 0)) - seq_index * tok

    far = n_head // 2
    rows_w = output_weight.shape[0]
    slice_w = rows_w // n_seq
    far_piece = swap(
        lax.dynamic_slice_in_dim(output_weight, seq_index * slice_w, slice_w, 0), "head", far
    )

    rates_next = shifted(step_rates[:, :slack], "seq", -1)
    rates_all = jnp.concatenate(
        [step_rates, rates_next, jnp.zeros((local_heads, cap - tok), f32)], axis=1
    )
    rates = lax.dynamic_slice_in_dim(rates_all, drift, cap, 1)
    valid = lax.broadcasted_iota(jnp.int32, (1, cap), 1) < frame_lengths[0]
    rates = jnp.transpose(jnp.where(valid, -rates, 0.0))
    grads = []
    for h in range(local_heads):
        cols = slice(h * HD, (h + 1) * HD)
        grads += head_grads(
            key_rows[:, cols],
            value_rows[:, cols],
            rates[:, h : h + 1],
            fast_gate[h].astype(bf16),
            fast_up[h].astype(bf16),
            fast_down[h].astype(bf16),
        )

    give_kv = WINDOW - drift
    got_k = shifted(lax.dynamic_slice_in_dim(key_rows, give_kv, WINDOW + slack, 0), "seq", 1)
    got_v = shifted(lax.dynamic_slice_in_dim(value_rows, give_kv, WINDOW + slack, 0), "seq", 1)
    got_q = shifted(lax.dynamic_slice_in_dim(query_rows, tok - drift, slack, 0), "seq", 1)

    paired = len(grads) % 2 == 0
    core_high = bit_of("seq", 1)
    fast = [
        weight[h] for h in range(local_heads) for weight in (fast_gate, fast_up, fast_down)
    ]
    if paired:
        half = len(grads) // 2
        low, high = jnp.stack(grads[:half]), jnp.stack(grads[half:])
        keep = jnp.where(core_high, high, low)
        give = jnp.where(core_high, low, high).astype(bf16)
        total = keep + swap(give, "seq", 1).astype(f32)
        total = seq_sum(total, masks)
        mine = jnp.where(core_high, jnp.stack(fast[half:]), jnp.stack(fast[:half]))
        new_mine = (mine - orthogonal(total)).astype(bf16)
        new_other = swap(new_mine, "seq", 1)
        news = list(jnp.where(core_high, new_other, new_mine)) + list(
            jnp.where(core_high, new_mine, new_other)
        )
    else:
        total = seq_sum(jnp.stack(grads), [1] + masks)
        news = list((jnp.stack(fast) - orthogonal(total)).astype(bf16))

    def settle(rows, got, lead):
        padded = jnp.concatenate([jnp.zeros((lead + slack, rows.shape[1]), rows.dtype), rows], 0)
        own = lax.dynamic_slice_in_dim(padded, slack - drift, lead + tok, 0)
        early = jnp.concatenate([got, jnp.zeros((tok - slack, rows.shape[1]), rows.dtype)], 0)
        slot = lax.broadcasted_iota(jnp.int32, (lead + tok, 1), 0)
        return jnp.where(slot < lead + drift, early, own)

    queries = settle(query_rows, got_q, 0)
    key_ext = settle(key_rows, got_k, WINDOW)
    value_ext = settle(value_rows, got_v, WINDOW)
    halo_live = seq_index > 0
    attention = [
        attend(
            queries[:, h * HD : (h + 1) * HD],
            key_ext[:, h * HD : (h + 1) * HD],
            value_ext[:, h * HD : (h + 1) * HD],
            halo_live,
            tok // 2,
        )
        for h in range(local_heads)
    ]

    orders = (masks, masks[::-1])
    far_weight = []
    for part in seq_gather(far_piece, masks):
        both = jnp.concatenate([part, swap(part, "seq", 1)], axis=0)
        far_weight.append(both.reshape(rows_w, -1))

    def arrival(rows, order):
        bits = (1,) + tuple(order[::-1])
        cut = rows.reshape((rows.shape[0],) + (2,) * len(bits) + (slice_w,))
        ranked = sorted(bits, reverse=True)
        cut = jnp.transpose(cut, (0,) + tuple(1 + ranked.index(m) for m in bits) + (len(bits) + 1,))
        for axis, mask in enumerate(bits):
            cut = jnp.where(bit_of("seq", mask), lax.rev(cut, (axis + 1,)), cut)
        return cut.reshape(rows.shape)

    combined = []
    for h in range(local_heads):
        gate, up, down = news[3 * h : 3 * h + 3]
        query = queries[:, h * HD : (h + 1) * HD]
        middle = (jax.nn.silu(mm(query, gate)) * mm(query, up)).astype(bf16)
        combined.append((attention[h].astype(f32) + mm(middle, down)).astype(bf16))
    combined = jnp.concatenate(combined, axis=1)

    keep, give = halves(combined, 0, bit_of("head", far))
    masks_head = []
    mask = far // 2
    while mask:
        masks_head.append(mask)
        mask //= 2
    if not masks_head:
        got = swap(give, "head", far)
        mixed = mm(keep, output_weight) + jnp.concatenate([mm(arrival(got, o), w) for o, w in zip(orders, far_weight)], 1)
        return mixed.astype(bf16)
    near_high = bit_of("head", masks_head[0])
    keep_stay, keep_send = halves(keep, 0, near_high)
    give_stay, give_send = halves(give, 0, near_high)
    got_send = swap(give_send, "head", far)
    got_stay = swap(give_stay, "head", far)

    def mix(near_rows, far_rows):
        return mm(near_rows, output_weight) + jnp.concatenate(
            [mm(arrival(far_rows, o), w) for o, w in zip(orders, far_weight)], 1
        )

    sent = swap(mix(keep_send, got_send).astype(bf16), "head", masks_head[0])
    mixed = mix(keep_stay, got_stay) + sent.astype(f32)
    for mask in masks_head[1:]:
        stay, leave = halves(mixed, 0, bit_of("head", mask))
        mixed = stay + swap(leave.astype(bf16), "head", mask).astype(f32)
    return mixed.astype(bf16)


def solution(mesh):
    return jax.shard_map(
        per_device,
        mesh=mesh,
        in_specs=(
            P("seq", "head"),
            P("seq", "head"),
            P("seq", "head"),
            P("seq"),
            P("head", "seq"),
            P("head", None, None),
            P("head", None, None),
            P("head", None, None),
            P("head", None),
        ),
        out_specs=P(("seq", "head"), None),
        check_vma=False,
    )
```

```python
import math

import jax
import jax.numpy as jnp
from jax import lax
from jax.experimental import pallas as pl
from jax.experimental.pallas import tpu as pltpu
from jax.sharding import PartitionSpec as P


HD = 512
WINDOW = 512
ITERS = 2

poly_first = 3.4445
poly_second = -4.775
poly_third = 2.0315
epsilon = 1e-07
masked_score = -1e30
bf16 = jnp.bfloat16
f32 = jnp.float32


def mm(a, b, dims=((1,), (0,))):
    return lax.dot_general(a, b, (dims, ((), ())), preferred_element_type=f32)


def swap(value, axis, mask):
    count = lax.axis_size(axis)
    return lax.ppermute(value, axis, [(i, i ^ mask) for i in range(count)])


def shifted(value, axis, steps):
    count = lax.axis_size(axis)
    first, last = (max(0, -steps), min(count, count - steps))
    return lax.ppermute(value, axis, [(i, i + steps) for i in range(first, last)])


def bit_of(axis, mask):
    return (lax.axis_index(axis) & mask) != 0


def halves(value, dim, high):
    half = value.shape[dim] // 2
    low_part = lax.slice_in_dim(value, 0, half, axis=dim)
    high_part = lax.slice_in_dim(value, half, 2 * half, axis=dim)
    return jnp.where(high, high_part, low_part), jnp.where(high, low_part, high_part)


def joined(mine, other, dim, high):
    return jnp.concatenate(
        [jnp.where(high, other, mine), jnp.where(high, mine, other)], axis=dim
    )


def reduce_over(value, masks, dim):
    for mask in masks:
        keep, give = halves(value, dim, bit_of("seq", mask))
        value = keep.astype(f32) + swap(give.astype(bf16), "seq", mask).astype(f32)
    return value.astype(bf16)


def gather_over(value, masks, dim):
    for mask in masks:
        value = joined(value, swap(value, "seq", mask), dim, bit_of("seq", mask))
    return value


def seq_sum(value, masks):
    half = value.shape[2] // 2
    parts = []
    for part, order in ((value[:, :, :half], masks), (value[:, :, half:], masks[::-1])):
        part = reduce_over(part, order, 1)
        parts.append(gather_over(part, order[::-1], 1))
    return jnp.concatenate(parts, axis=2)


def update_kernel(grad_ref, fast_ref, out_ref):
    gradient = grad_ref[0].astype(f32)
    norm_value = jnp.sqrt(jnp.sum(gradient * gradient, keepdims=True))
    current = gradient / (norm_value + epsilon)
    for _ in range(ITERS):
        low = current.astype(bf16)
        gram = mm(low, low, ((1,), (1,)))
        gram_low = gram.astype(bf16)
        poly = poly_second * gram + poly_third * mm(gram_low, gram_low)
        current = poly_first * current + mm(poly.astype(bf16), low)
    out_ref[0] = (fast_ref[0] - current).astype(bf16)


def updated(fast, total):
    count, rows, cols = total.shape
    block = pl.BlockSpec((1, rows, cols), lambda i: (i, 0, 0))
    return pl.pallas_call(
        update_kernel,
        grid=(count,),
        in_specs=[block, block],
        out_specs=block,
        out_shape=jax.ShapeDtypeStruct(total.shape, bf16),
        compiler_params=pltpu.CompilerParams(dimension_semantics=("arbitrary",)),
        cost_estimate=pl.CostEstimate(
            flops=count * ITERS * 6 * rows * rows * cols,
            bytes_accessed=count * rows * cols * 8,
            transcendentals=0,
        ),
        name="update",
    )(total, fast)


def head_grads(key, value, rate, gate, up, down):
    pre_gate = mm(key, gate)
    pre_up = mm(key, up)
    sigma = jax.nn.sigmoid(pre_gate)
    activated = pre_gate * sigma
    inner = (activated * pre_up).astype(bf16)
    target = (rate * value.astype(f32)).astype(bf16)
    grad_down = mm(inner, target, ((0,), (0,)))
    back = mm(target, down, ((1,), (1,)))
    back_up = (back * activated).astype(bf16)
    back_gate = (back * pre_up * (sigma * (1.0 + pre_gate * (1.0 - sigma)))).astype(bf16)
    return [mm(key, back_gate, ((0,), (0,))), mm(key, back_up, ((0,), (0,))), grad_down]


def attend(query, key_ext, value_ext, halo_live, block_rows):
    scale_factor = 1.0 / math.sqrt(HD)
    pieces = []
    for first in range(0, query.shape[0], block_rows):
        span = block_rows + WINDOW
        scores = (
            mm(query[first : first + block_rows], key_ext[first : first + span], ((1,), (1,)))
            * scale_factor
        )
        query_pos = first + lax.broadcasted_iota(jnp.int32, (block_rows, 1), 0)
        key_pos = first - WINDOW + lax.broadcasted_iota(jnp.int32, (1, span), 1)
        allowed = (
            (key_pos <= query_pos) & (key_pos > query_pos - WINDOW) & ((key_pos >= 0) | halo_live)
        )
        scores = jnp.where(allowed, scores, masked_score)
        weights = jnp.exp(scores - jnp.max(scores, axis=1, keepdims=True))
        totals = jnp.sum(weights, axis=1, keepdims=True)
        summed = mm(weights.astype(bf16), value_ext[first : first + span])
        pieces.append((summed / totals).astype(bf16))
    return jnp.concatenate(pieces, axis=0)


def per_device(
    query_rows,
    key_rows,
    value_rows,
    frame_lengths,
    step_rates,
    fast_gate,
    fast_up,
    fast_down,
    output_weight,
):
    local_heads = query_rows.shape[1] // HD
    cap = query_rows.shape[0]
    tok = step_rates.shape[1]
    slack = cap - tok
    n_seq, n_head = lax.axis_size("seq"), lax.axis_size("head")
    seq_index = lax.axis_index("seq")
    masks = [1 << b for b in range(1, n_seq.bit_length() - 1)]

    lengths = lax.all_gather(frame_lengths, "seq", tiled=True)
    before = lax.broadcasted_iota(jnp.int32, (n_seq,), 0) < seq_index
    drift = jnp.sum(jnp.where(before, lengths, 0)) - seq_index * tok

    far = n_head // 2
    rows_w = output_weight.shape[0]
    slice_w = rows_w // n_seq
    far_piece = swap(
        lax.dynamic_slice_in_dim(output_weight, seq_index * slice_w, slice_w, 0), "head", far
    )

    rates_next = shifted(step_rates[:, :slack], "seq", -1)
    rates_all = jnp.concatenate(
        [step_rates, rates_next, jnp.zeros((local_heads, cap - tok), f32)], axis=1
    )
    rates = lax.dynamic_slice_in_dim(rates_all, drift, cap, 1)
    valid = lax.broadcasted_iota(jnp.int32, (1, cap), 1) < frame_lengths[0]
    rates = jnp.transpose(jnp.where(valid, -rates, 0.0))
    grads = []
    for h in range(local_heads):
        cols = slice(h * HD, (h + 1) * HD)
        grads += head_grads(
            key_rows[:, cols],
            value_rows[:, cols],
            rates[:, h : h + 1],
            fast_gate[h].astype(bf16),
            fast_up[h].astype(bf16),
            fast_down[h].astype(bf16),
        )

    give_kv = WINDOW - drift
    got_k = shifted(lax.dynamic_slice_in_dim(key_rows, give_kv, WINDOW + slack, 0), "seq", 1)
    got_v = shifted(lax.dynamic_slice_in_dim(value_rows, give_kv, WINDOW + slack, 0), "seq", 1)
    got_q = shifted(lax.dynamic_slice_in_dim(query_rows, tok - drift, slack, 0), "seq", 1)

    paired = len(grads) % 2 == 0
    core_high = bit_of("seq", 1)
    fast = [
        weight[h] for h in range(local_heads) for weight in (fast_gate, fast_up, fast_down)
    ]
    if paired:
        half = len(grads) // 2
        low, high = jnp.stack(grads[:half]), jnp.stack(grads[half:])
        keep = jnp.where(core_high, high, low)
        give = jnp.where(core_high, low, high).astype(bf16)
        total = keep + swap(give, "seq", 1).astype(f32)
        total = seq_sum(total, masks)
        mine = jnp.where(core_high, jnp.stack(fast[half:]), jnp.stack(fast[:half]))
        new_mine = updated(mine, total)
        new_other = swap(new_mine, "seq", 1)
        news = list(jnp.where(core_high, new_other, new_mine)) + list(
            jnp.where(core_high, new_mine, new_other)
        )
    else:
        total = seq_sum(jnp.stack(grads), [1] + masks)
        news = list(updated(jnp.stack(fast), total))

    def settle(rows, got, lead):
        padded = jnp.concatenate([jnp.zeros((lead + slack, rows.shape[1]), rows.dtype), rows], 0)
        own = lax.dynamic_slice_in_dim(padded, slack - drift, lead + tok, 0)
        early = jnp.concatenate([got, jnp.zeros((tok - slack, rows.shape[1]), rows.dtype)], 0)
        slot = lax.broadcasted_iota(jnp.int32, (lead + tok, 1), 0)
        return jnp.where(slot < lead + drift, early, own)

    queries = settle(query_rows, got_q, 0)
    key_ext = settle(key_rows, got_k, WINDOW)
    value_ext = settle(value_rows, got_v, WINDOW)
    halo_live = seq_index > 0
    attention = [
        attend(
            queries[:, h * HD : (h + 1) * HD],
            key_ext[:, h * HD : (h + 1) * HD],
            value_ext[:, h * HD : (h + 1) * HD],
            halo_live,
            tok // 2,
        )
        for h in range(local_heads)
    ]

    far_piece = lax.optimization_barrier((far_piece, total))[0]
    far_pieces = [far_piece] + [swap(far_piece, "seq", m) for m in range(2, n_seq, 2)]

    out_col = lax.broadcasted_iota(jnp.int32, (1, rows_w), 1)
    place = out_col // slice_w
    rank = jnp.where(place < n_seq // 2, 2 * place, 2 * place - n_seq + 1)
    source = (seq_index ^ rank) * slice_w + out_col % slice_w
    arrival = (lax.broadcasted_iota(jnp.int32, (rows_w, rows_w), 0) == source).astype(bf16)

    combined = []
    for h in range(local_heads):
        gate, up, down = news[3 * h : 3 * h + 3]
        query = queries[:, h * HD : (h + 1) * HD]
        middle = (jax.nn.silu(mm(query, gate)) * mm(query, up)).astype(bf16)
        combined.append((attention[h].astype(f32) + mm(middle, down)).astype(bf16))
    combined = jnp.concatenate(combined, axis=1)

    near_core = jnp.concatenate(far_pieces, axis=0)
    far_weight = (near_core, swap(near_core, "seq", 1))
    keep, give = halves(combined, 0, bit_of("head", far))
    give = mm(give, arrival).astype(bf16)
    masks_head = []
    mask = far // 2
    while mask:
        masks_head.append(mask)
        mask //= 2

    def mix(near_rows, far_rows):
        middle = far_rows.shape[1] // 2
        return (
            mm(near_rows, output_weight)
            + mm(far_rows[:, :middle], far_weight[0])
            + mm(far_rows[:, middle:], far_weight[1])
        )

    if not masks_head:
        return mix(keep, swap(give, "head", far)).astype(bf16)

    def mix(near_rows, far_rows):
        middle = far_rows.shape[1] // 2
        return (
            mm(near_rows, output_weight)
            + mm(far_rows[:, :middle], far_weight[0])
            + mm(far_rows[:, middle:], far_weight[1])
        )

    if not masks_head:
        return mix(keep, swap(give, "head", far)).astype(bf16)
    near_high = bit_of("head", masks_head[0])
    keep_stay, keep_send = halves(keep, 0, near_high)
    give_stay, give_send = halves(give, 0, near_high)
    got_send = swap(give_send, "head", far)
    give_stay, got_send = lax.optimization_barrier((give_stay, got_send))
    got_stay = swap(give_stay, "head", far)
    partial = mix(keep_send, got_send).astype(bf16)
    sent = swap(partial, "head", masks_head[0])
    own = lax.optimization_barrier(mix(keep_stay, got_stay))
    mixed = own + sent.astype(f32)
    for mask in masks_head[1:]:
        stay, leave = halves(mixed, 0, bit_of("head", mask))
        mixed = stay + swap(leave.astype(bf16), "head", mask).astype(f32)
    return mixed.astype(bf16)


def solution(mesh):
    return jax.shard_map(
        per_device,
        mesh=mesh,
        in_specs=(
            P("seq", "head"),
            P("seq", "head"),
            P("seq", "head"),
            P("seq"),
            P("head", "seq"),
            P("head", None, None),
            P("head", None, None),
            P("head", None, None),
            P("head", None),
        ),
        out_specs=P(("seq", "head"), None),
        check_vma=False,
    )
```

```python
import math

import jax
import jax.numpy as jnp
from jax import lax
from jax.experimental import pallas as pl
from jax.experimental.pallas import tpu as pltpu
from jax.sharding import PartitionSpec as P


HD = 512
WINDOW = 512
ITERS = 2

poly_first = 3.4445
poly_second = -4.775
poly_third = 2.0315
epsilon = 1e-07
masked_score = -1e30
bf16 = jnp.bfloat16
f32 = jnp.float32


def mm(a, b, dims=((1,), (0,))):
    return lax.dot_general(a, b, (dims, ((), ())), preferred_element_type=f32)


def swap(value, axis, mask):
    count = lax.axis_size(axis)
    return lax.ppermute(value, axis, [(i, i ^ mask) for i in range(count)])


def shifted(value, axis, steps):
    count = lax.axis_size(axis)
    first, last = (max(0, -steps), min(count, count - steps))
    return lax.ppermute(value, axis, [(i, i + steps) for i in range(first, last)])


def bit_of(axis, mask):
    return (lax.axis_index(axis) & mask) != 0


def halves(value, dim, high):
    half = value.shape[dim] // 2
    low_part = lax.slice_in_dim(value, 0, half, axis=dim)
    high_part = lax.slice_in_dim(value, half, 2 * half, axis=dim)
    return jnp.where(high, high_part, low_part), jnp.where(high, low_part, high_part)


def joined(mine, other, dim, high):
    return jnp.concatenate(
        [jnp.where(high, other, mine), jnp.where(high, mine, other)], axis=dim
    )


def reduce_over(value, masks, dim):
    for mask in masks:
        keep, give = halves(value, dim, bit_of("seq", mask))
        value = keep.astype(f32) + swap(give.astype(bf16), "seq", mask).astype(f32)
    return value.astype(bf16)


def gather_over(value, masks, dim):
    for mask in masks:
        value = joined(value, swap(value, "seq", mask), dim, bit_of("seq", mask))
    return value


def seq_sum(value, masks):
    half = value.shape[2] // 2
    parts = []
    for part, order in ((value[:, :, :half], masks), (value[:, :, half:], masks[::-1])):
        part = reduce_over(part, order, 1)
        parts.append(gather_over(part, order[::-1], 1))
    return jnp.concatenate(parts, axis=2)


def update_kernel(grad_ref, fast_ref, out_ref):
    gradient = grad_ref[0].astype(f32)
    norm_value = jnp.sqrt(jnp.sum(gradient * gradient, keepdims=True))
    current = gradient / (norm_value + epsilon)
    for _ in range(ITERS):
        low = current.astype(bf16)
        gram = mm(low, low, ((1,), (1,)))
        gram_low = gram.astype(bf16)
        poly = poly_second * gram + poly_third * mm(gram_low, gram_low)
        current = poly_first * current + mm(poly.astype(bf16), low)
    out_ref[0] = (fast_ref[0] - current).astype(bf16)


def updated(fast, total):
    count, rows, cols = total.shape
    block = pl.BlockSpec((1, rows, cols), lambda i: (i, 0, 0))
    return pl.pallas_call(
        update_kernel,
        grid=(count,),
        in_specs=[block, block],
        out_specs=block,
        out_shape=jax.ShapeDtypeStruct(total.shape, bf16),
        compiler_params=pltpu.CompilerParams(dimension_semantics=("arbitrary",)),
        cost_estimate=pl.CostEstimate(
            flops=count * ITERS * 6 * rows * rows * cols,
            bytes_accessed=count * rows * cols * 8,
            transcendentals=0,
        ),
        name="update",
    )(total, fast)


def head_grads(key, value, rate, gate, up, down):
    pre_gate = mm(key, gate)
    pre_up = mm(key, up)
    sigma = jax.nn.sigmoid(pre_gate)
    activated = pre_gate * sigma
    inner = (activated * pre_up).astype(bf16)
    target = (rate * value.astype(f32)).astype(bf16)
    grad_down = mm(inner, target, ((0,), (0,)))
    back = mm(target, down, ((1,), (1,)))
    back_up = (back * activated).astype(bf16)
    back_gate = (back * pre_up * (sigma * (1.0 + pre_gate * (1.0 - sigma)))).astype(bf16)
    return [mm(key, back_gate, ((0,), (0,))), mm(key, back_up, ((0,), (0,))), grad_down]


def attend(query, key_ext, value_ext, halo_live, block_rows):
    scale_factor = 1.0 / math.sqrt(HD)
    pieces = []
    for first in range(0, query.shape[0], block_rows):
        span = block_rows + WINDOW
        scores = (
            mm(query[first : first + block_rows], key_ext[first : first + span], ((1,), (1,)))
            * scale_factor
        )
        query_pos = first + lax.broadcasted_iota(jnp.int32, (block_rows, 1), 0)
        key_pos = first - WINDOW + lax.broadcasted_iota(jnp.int32, (1, span), 1)
        allowed = (
            (key_pos <= query_pos) & (key_pos > query_pos - WINDOW) & ((key_pos >= 0) | halo_live)
        )
        scores = jnp.where(allowed, scores, masked_score)
        weights = jnp.exp(scores - jnp.max(scores, axis=1, keepdims=True))
        totals = jnp.sum(weights, axis=1, keepdims=True)
        summed = mm(weights.astype(bf16), value_ext[first : first + span])
        pieces.append((summed / totals).astype(bf16))
    return jnp.concatenate(pieces, axis=0)


def per_device(
    query_rows,
    key_rows,
    value_rows,
    frame_lengths,
    step_rates,
    fast_gate,
    fast_up,
    fast_down,
    output_weight,
):
    local_heads = query_rows.shape[1] // HD
    cap = query_rows.shape[0]
    tok = step_rates.shape[1]
    slack = cap - tok
    n_seq, n_head = lax.axis_size("seq"), lax.axis_size("head")
    seq_index = lax.axis_index("seq")
    masks = [1 << b for b in range(1, n_seq.bit_length() - 1)]

    running = frame_lengths
    step = 1
    while step < n_seq:
        running = running + shifted(running, "seq", step)
        step *= 2
    drift = (running - frame_lengths)[0] - seq_index * tok

    far = n_head // 2
    rows_w = output_weight.shape[0]
    slice_w = rows_w // n_seq
    far_piece = swap(
        lax.dynamic_slice_in_dim(output_weight, seq_index * slice_w, slice_w, 0), "head", far
    )

    rates_next = shifted(step_rates[:, :slack], "seq", -1)
    rates_all = jnp.concatenate(
        [step_rates, rates_next, jnp.zeros((local_heads, cap - tok), f32)], axis=1
    )
    rates = lax.dynamic_slice_in_dim(rates_all, drift, cap, 1)
    valid = lax.broadcasted_iota(jnp.int32, (1, cap), 1) < frame_lengths[0]
    rates = jnp.transpose(jnp.where(valid, -rates, 0.0))
    grads = []
    for h in range(local_heads):
        cols = slice(h * HD, (h + 1) * HD)
        grads += head_grads(
            key_rows[:, cols],
            value_rows[:, cols],
            rates[:, h : h + 1],
            fast_gate[h].astype(bf16),
            fast_up[h].astype(bf16),
            fast_down[h].astype(bf16),
        )

    give_kv = WINDOW - drift
    got_k = shifted(lax.dynamic_slice_in_dim(key_rows, give_kv, WINDOW + slack, 0), "seq", 1)
    got_v = shifted(lax.dynamic_slice_in_dim(value_rows, give_kv, WINDOW + slack, 0), "seq", 1)
    got_q = shifted(lax.dynamic_slice_in_dim(query_rows, tok - drift, slack, 0), "seq", 1)

    paired = len(grads) % 2 == 0
    core_high = bit_of("seq", 1)
    fast = [
        weight[h] for h in range(local_heads) for weight in (fast_gate, fast_up, fast_down)
    ]
    if paired:
        half = len(grads) // 2
        low, high = jnp.stack(grads[:half]), jnp.stack(grads[half:])
        keep = jnp.where(core_high, high, low)
        give = jnp.where(core_high, low, high).astype(bf16)
        total = keep + swap(give, "seq", 1).astype(f32)
        total = seq_sum(total, masks)
        mine = jnp.where(core_high, jnp.stack(fast[half:]), jnp.stack(fast[:half]))
        new_mine = updated(mine, total)
        new_other = swap(new_mine, "seq", 1)
        news = list(jnp.where(core_high, new_other, new_mine)) + list(
            jnp.where(core_high, new_mine, new_other)
        )
    else:
        total = seq_sum(jnp.stack(grads), [1] + masks)
        news = list(updated(jnp.stack(fast), total))

    def settle(rows, got, lead):
        padded = jnp.concatenate([jnp.zeros((lead + slack, rows.shape[1]), rows.dtype), rows], 0)
        own = lax.dynamic_slice_in_dim(padded, slack - drift, lead + tok, 0)
        early = jnp.concatenate([got, jnp.zeros((tok - slack, rows.shape[1]), rows.dtype)], 0)
        slot = lax.broadcasted_iota(jnp.int32, (lead + tok, 1), 0)
        return jnp.where(slot < lead + drift, early, own)

    queries = settle(query_rows, got_q, 0)
    key_ext = settle(key_rows, got_k, WINDOW)
    value_ext = settle(value_rows, got_v, WINDOW)
    halo_live = seq_index > 0
    attention = [
        attend(
            queries[:, h * HD : (h + 1) * HD],
            key_ext[:, h * HD : (h + 1) * HD],
            value_ext[:, h * HD : (h + 1) * HD],
            halo_live,
            tok // 2,
        )
        for h in range(local_heads)
    ]

    far_piece = lax.optimization_barrier((far_piece, total))[0]
    far_pieces = [far_piece] + [swap(far_piece, "seq", m) for m in range(2, n_seq, 2)]

    out_col = lax.broadcasted_iota(jnp.int32, (1, rows_w), 1)
    place = out_col // slice_w
    rank = jnp.where(place < n_seq // 2, 2 * place, 2 * place - n_seq + 1)
    source = (seq_index ^ rank) * slice_w + out_col % slice_w
    arrival = (lax.broadcasted_iota(jnp.int32, (rows_w, rows_w), 0) == source).astype(bf16)

    combined = []
    for h in range(local_heads):
        gate, up, down = news[3 * h : 3 * h + 3]
        query = queries[:, h * HD : (h + 1) * HD]
        middle = (jax.nn.silu(mm(query, gate)) * mm(query, up)).astype(bf16)
        combined.append((attention[h].astype(f32) + mm(middle, down)).astype(bf16))
    combined = jnp.concatenate(combined, axis=1)

    near_core = jnp.concatenate(far_pieces, axis=0)
    far_weight = (near_core, swap(near_core, "seq", 1))
    keep, give = halves(combined, 0, bit_of("head", far))
    give = mm(give, arrival).astype(bf16)
    masks_head = []
    mask = far // 2
    while mask:
        masks_head.append(mask)
        mask //= 2

    def mix(near_rows, far_rows):
        middle = far_rows.shape[1] // 2
        return (
            mm(near_rows, output_weight)
            + mm(far_rows[:, :middle], far_weight[0])
            + mm(far_rows[:, middle:], far_weight[1])
        )

    if not masks_head:
        return mix(keep, swap(give, "head", far)).astype(bf16)

    def mix(near_rows, far_rows):
        middle = far_rows.shape[1] // 2
        return (
            mm(near_rows, output_weight)
            + mm(far_rows[:, :middle], far_weight[0])
            + mm(far_rows[:, middle:], far_weight[1])
        )

    if not masks_head:
        return mix(keep, swap(give, "head", far)).astype(bf16)
    near = masks_head[0]
    near_high = bit_of("head", near)
    keep_stay, keep_send = halves(keep, 0, near_high)
    give_stay, give_send = halves(give, 0, near_high)
    cut = keep_send.shape[0] // 2
    got_0 = swap(give_send[:cut], "head", far)
    give_1, got_0 = lax.optimization_barrier((give_send[cut:], got_0))
    got_1 = swap(give_1, "head", far)
    give_stay, got_1 = lax.optimization_barrier((give_stay, got_1))
    got_2 = swap(give_stay, "head", far)
    partial_0 = mix(keep_send[:cut], got_0).astype(bf16)
    sent_0 = swap(partial_0, "head", near)
    partial_1 = mix(keep_send[cut:], got_1).astype(bf16)
    sent_1 = swap(partial_1, "head", near)
    own = lax.optimization_barrier(mix(keep_stay, got_2))
    mixed = own + jnp.concatenate([sent_0, sent_1], axis=0).astype(f32)
    for mask in masks_head[1:]:
        stay, leave = halves(mixed, 0, bit_of("head", mask))
        mixed = stay + swap(leave.astype(bf16), "head", mask).astype(f32)
    return mixed.astype(bf16)


def solution(mesh):
    return jax.shard_map(
        per_device,
        mesh=mesh,
        in_specs=(
            P("seq", "head"),
            P("seq", "head"),
            P("seq", "head"),
            P("seq"),
            P("head", "seq"),
            P("head", None, None),
            P("head", None, None),
            P("head", None, None),
            P("head", None),
        ),
        out_specs=P(("seq", "head"), None),
        check_vma=False,
    )
```
